32 devices in a mesh: comp: 8 (over y, x, core), tile: 4 (over z).
Axes of the slice: x: 2, y: 2, z: 4, core: 2. Of those that a mesh axis runs over, the one named last changes fastest.
Arguments:
- spectrum: bfloat16 [1296, 128, 1024], P('comp', 'tile'), may hold values from 0.049804688 to 1
- courant_x: float32 [1296], replicated, may hold values from -0.45 to 0.45
- courant_y: float32 [1296], replicated, may hold values from -0.45 to 0.45
- growth: float32 [1296], replicated, may hold values from 0.02 to 0.2
- dissipation: float32 [1296], replicated, may hold values from 0.1 to 1
- bin_width: float32 [1296], replicated, may hold values from 0.00038580247 to 0.0030864198
- transfer: bfloat16 [1296, 1296], replicated, may hold values from -0.15625 to 0.15625
- stress_weights: float32 [2, 1296], replicated, may hold values from -0.15625 to 0.15625
- orbital_weights: float32 [1296], replicated, may hold values from 0.000154321 to 0.0015432099
- wind: float32 [128, 1024], P('tile', 'comp'), may hold values from 1 to 10
- wave_wet: int32 [128, 1024], P('tile', 'comp'), may hold values 0 or 1
- owner: int32 [4, 8, 32, 128, 1], P('tile', 'comp'), may hold values from 0 to 31; in each aligned block of 4096 rows (0 to 4095, 4096 to 8191, ..., all dimensions but the last counted through in order) at most 384 rows name the same one
- cell_index: int32 [4, 8, 32, 128], P('tile', 'comp'), may hold values from 0 to 2047
- current_stress: float32 [2, 64, 1024], P(None, 'tile', 'comp'), may hold values from -3 to 3
- sediment: float32 [4, 64, 1024], P(None, 'tile', 'comp'), may hold values from 0.1 to 2
- metals: float32 [4, 64, 1024], P(None, 'tile', 'comp'), may hold values from 0.1 to 2
- bed_class: int32 [64, 1024], P('tile', 'comp'), may hold values from 0 to 3
- roms_wet: int32 [64, 1024], P('tile', 'comp'), may hold values 0 or 1
- class_props: float32 [3, 4], replicated, may hold values from 0.2 to 0.8
- partition: float32 [4, 4], replicated, may hold values from 0.3 to 3
Outputs:
- spectrum_new: bfloat16 [1296, 128, 1024], P(None, 'tile', 'comp')
- sediment_new: float32 [4, 64, 1024], P(None, 'tile', 'comp')
- dissolved: float32 [4, 64, 1024], P(None, 'tile', 'comp')
- sorbed: float32 [4, 64, 1024], P(None, 'tile', 'comp')
The draws below stay inside these ranges and needn't reach their ends.
Inputs may be any that keep to these rules, and one draw needn't show every extreme that they name: `owner`: within each aligned block of 4096 points (one device's points, in order), no tile is named more than 384 times, a bound that some block reaches.
All inputs are finite; a program needn't handle non-finite values. No bound on the sum of `wave_wet` or of `roms_wet` on one device may be relied on, other than what follows from the above.
Results may differ from the reference program's by a relative error of at most 0.0049.
Values may be sent and summed in bfloat16 or wider, within the bound.
A program may use at most 192 MiB of HBM per device.

```python
import math
import jax
import jax.numpy as jnp
import numpy as np
from jax import lax

NSED = 4
NMET = 4
ROWS_DEV = 32
COLS_DEV = 128
RR = 16
RC = 128
K = 1296
GX = 128
GY = 1024
RX = 64
RY = 1024
CELLS = 2048
CAP = 384
N_COMP = 8
N_TILE = 4
DEVICES = 32


def place_ends(drawn, rng, least, top_value):
    extent = drawn.shape
    spot = [jax.random.randint(jax.random.fold_in(rng, axis), (), 0, extent[axis]) for axis in range(len(extent))]
    drawn = drawn.at[tuple(spot)].set(least)
    longest = extent.index(max(extent))
    spot[longest] = (spot[longest] + 1) % extent[longest]
    return drawn.at[tuple(spot)].set(top_value)


def levels(rng, extent, cuts, smallest, high):
    factor_of = 1.0
    for position, blocks in cuts:
        steps = jax.random.uniform(jax.random.fold_in(jax.random.fold_in(rng, 6), position), (blocks,), jnp.float32, smallest / len(cuts), high / len(cuts))
        factor_of = factor_of * jnp.repeat(jnp.exp(steps), extent[position] // blocks).reshape((-1,) + (1,) * (len(extent) - 1 - position))
    return factor_of


def routed_block(key, own, number, rows, number_of, top, bound, slope):
    sequence = jax.random.permutation(key, number_of)
    heavy_load, common = load_shares(number_of, rows * top, bound, slope, True), load_shares(number_of, rows * top, bound, slope, False)
    places = jnp.arange(number_of)

    def named(tallies, turn):
        used = int((tallies > 0).sum())
        fixed = max(1, used // 4)
        shifted = fixed + (places - fixed + turn * (used - fixed)) % max(1, number_of - fixed)
        return jnp.zeros((number_of,), jnp.int32).at[sequence[jnp.where(places < fixed, places, shifted)]].set(jnp.asarray(tallies, jnp.int32))

    tallies = jnp.where(number % 4 == 0, named(heavy_load, number // 4), named(common, number - number // 4 - 1))
    mixed = jax.random.permutation(jax.random.fold_in(own, 3), number_of)
    donor, taker = mixed[0:number_of // 2 * 2:2], mixed[1:number_of // 2 * 2:2]
    room = jnp.minimum(tallies[donor] - 1, bound - tallies[taker]) // 2
    room = jnp.where((donor == sequence[0]) | (taker == sequence[0]) | (tallies[taker] == 0), 0, jnp.maximum(room, 0))
    shifted = jax.random.randint(jax.random.fold_in(own, 4), (number_of // 2,), 0, 1 << 20) % (room + 1)
    tallies = tallies.at[donor].add(-shifted).at[taker].add(shifted)
    items = jnp.searchsorted(jnp.cumsum(tallies), jnp.arange(rows * top), side="right").astype(jnp.int32)
    table = items.reshape(top, rows).T
    table = table[jax.random.permutation(jax.random.fold_in(own, 1), rows)]
    turn = jax.random.randint(jax.random.fold_in(own, 2), (rows, 1), 0, top)
    return jnp.take_along_axis(table, (jnp.arange(top)[None, :] + turn) % top, axis=1)


def load_shares(amount, total, most, slope, full):
    weights = [(1 << 20) // math.isqrt(rank ** slope) + 1 for rank in range(1, amount + 1)]
    largest = most if full else min(most, max(-(-total // amount), total * weights[0] // sum(weights)))
    least = 1 if total - largest >= amount - 1 else 0
    given, rest = [largest] + [least] * (amount - 1), total - largest - least * (amount - 1)
    while rest > 0:
        candidates = [i for i in range(1, amount) if given[i] < largest] or [i for i in range(1, amount) if given[i] < most]
        whole, remaining = sum([weights[i] for i in candidates]), rest
        for i in candidates:
            extra = min(most - given[i], max(1, remaining * weights[i] // whole), rest)
            given[i] = given[i] + extra
            rest = rest - extra
    return np.array(given)


def scatter_about(key, extent, deviation, bound, shards=(), held_as=jnp.bfloat16):
    level = levels(key, extent, shards, -0.22, 0.18) if shards else 1.0
    entries = jax.random.normal(key, extent, jnp.float32) * deviation * level
    return jnp.minimum(jnp.maximum(entries, -bound), bound).astype(held_as)


def setup_inputs(seed: int = 0) -> dict:
    key_of = jax.random.split(jax.random.key(seed), 21)
    spectrum = jnp.clip(0.049804688 + 0.9501953 * jax.random.uniform(key_of[0], (K, GX, GY), jnp.float32) ** levels(key_of[0], (K, GX, GY), ((0, 8), (1, 4)), -0.2, 0.2), 0.049804688, 1.0).astype(jnp.bfloat16)
    courant_x = jnp.clip(jax.random.uniform(key_of[1], (K,), jnp.float32, -0.45, 0.45), -0.45, 0.45)
    courant_y = jnp.clip(jax.random.uniform(key_of[2], (K,), jnp.float32, -0.45, 0.45), -0.45, 0.45)
    growth = jnp.clip(jnp.exp(jax.random.uniform(key_of[3], (K,), jnp.float32, math.log(0.02), math.log(0.2))), 0.02, 0.2)
    dissipation = jnp.clip(jnp.exp(jax.random.uniform(key_of[4], (K,), jnp.float32, math.log(0.1), math.log(1.0))), 0.1, 1.0)
    bin_width = jnp.clip(jnp.exp(jax.random.uniform(key_of[5], (K,), jnp.float32, math.log(0.00038580247), math.log(0.0030864198))), 0.00038580247, 0.0030864198)
    transfer = scatter_about(key_of[6], (K, K), K ** -0.5, 0.15625)
    stress_weights = scatter_about(key_of[7], (2, K), K ** -0.5, 0.15625, (), jnp.float32)
    orbital_weights = jnp.clip(jnp.exp(jax.random.uniform(key_of[8], (K,), jnp.float32, math.log(0.000154321), math.log(0.0015432099))), 0.000154321, 0.0015432099)
    wind = jnp.clip(jnp.exp(math.log(10.0) - 2.3025851 * jax.random.uniform(key_of[9], (GX, GY), jnp.float32) ** levels(key_of[9], (GX, GY), ((0, 4), (1, 8)), -0.2, 0.2)), 1.0, 10.0)
    wave_wet = place_ends((jax.random.randint(key_of[10], (GX, GY), 0, 5) < 4).astype(jnp.int32), jax.random.fold_in(key_of[10], 1), 0, 1)
    owner_keys = jax.random.split(jax.random.fold_in(key_of[11], 1), N_TILE * N_COMP * ROWS_DEV * COLS_DEV // (ROWS_DEV * COLS_DEV))
    owner_turns = jax.random.permutation(jax.random.fold_in(key_of[11], 3), N_TILE * N_COMP * ROWS_DEV * COLS_DEV // (ROWS_DEV * COLS_DEV))
    owner = jax.vmap(lambda own, number: routed_block(jax.random.fold_in(key_of[11], 2), own, number, ROWS_DEV * COLS_DEV, DEVICES, 1, CAP, 2))(owner_keys, owner_turns).reshape((N_TILE, N_COMP, ROWS_DEV, COLS_DEV, 1))
    cell_index = place_ends(jax.random.randint(key_of[12], (N_TILE, N_COMP, ROWS_DEV, COLS_DEV), 0, CELLS), jax.random.fold_in(key_of[12], 1), 0, CELLS - 1).astype(jnp.int32)
    current_stress = scatter_about(key_of[13], (2, RX, RY), 0.5, 3.0, ((1, 4), (2, 8)), jnp.float32)
    sediment = jnp.clip(jnp.exp(math.log(2.0) - 2.9957323 * jax.random.uniform(key_of[14], (NSED, RX, RY), jnp.float32) ** levels(key_of[14], (NSED, RX, RY), ((1, 4), (2, 8)), -0.2, 0.2)), 0.1, 2.0)
    metals = jnp.clip(jnp.exp(math.log(2.0) - 2.9957323 * jax.random.uniform(key_of[15], (NMET, RX, RY), jnp.float32) ** levels(key_of[15], (NMET, RX, RY), ((1, 4), (2, 8)), -0.2, 0.2)), 0.1, 2.0)
    bed_class = place_ends(jax.random.randint(key_of[16], (RX, RY), 0, NSED), jax.random.fold_in(key_of[16], 1), 0, NSED - 1).astype(jnp.int32)
    roms_wet = place_ends((jax.random.randint(key_of[17], (RX, RY), 0, 8) < 7).astype(jnp.int32), jax.random.fold_in(key_of[17], 1), 0, 1)
    class_props = jnp.clip(jnp.exp(jax.random.uniform(key_of[18], (3, NSED), jnp.float32, math.log(0.2), math.log(0.8))), 0.2, 0.8)
    partition = jnp.clip(jnp.exp(jax.random.uniform(key_of[19], (NMET, NSED), jnp.float32, math.log(0.3), math.log(3.0))), 0.3, 3.0)
    return {"spectrum": spectrum, "courant_x": courant_x, "courant_y": courant_y, "growth": growth, "dissipation": dissipation, "bin_width": bin_width, "transfer": transfer, "stress_weights": stress_weights, "orbital_weights": orbital_weights, "wind": wind, "wave_wet": wave_wet, "owner": owner, "cell_index": cell_index, "current_stress": current_stress, "sediment": sediment, "metals": metals, "bed_class": bed_class, "roms_wet": roms_wet, "class_props": class_props, "partition": partition}


WAVE_STEP = 0.5
SEDIMENT_STEP = 1.0
DIFFUSION = 0.2

def upwind(padded, speed_x, speed_y):
    centre = padded[..., 1:-1, 1:-1]
    north = padded[..., :-2, 1:-1]
    south = padded[..., 2:, 1:-1]
    west = padded[..., 1:-1, :-2]
    east = padded[..., 1:-1, 2:]
    return centre - jnp.maximum(speed_x, 0.0) * (centre - north) - jnp.minimum(speed_x, 0.0) * (south - centre) - jnp.maximum(speed_y, 0.0) * (centre - west) - jnp.minimum(speed_y, 0.0) * (east - centre)

def diffuse(fields, wetness):
    padded = jnp.pad(fields, ((0, 0), (1, 1), (1, 1)))
    centre = padded[:, 1:-1, 1:-1]
    beside_all = padded[:, :-2, 1:-1] + padded[:, 2:, 1:-1] + padded[:, 1:-1, :-2] + padded[:, 1:-1, 2:]
    return wetness * (centre + DIFFUSION * (beside_all - 4.0 * centre))

def reference(spectrum, courant_x, courant_y, growth, dissipation, bin_width, transfer, stress_weights, orbital_weights, wind, wave_wet, owner, cell_index, current_stress, sediment, metals, bed_class, roms_wet, class_props, partition):

    def propagate_one(items):
        field, speed_x, speed_y = items
        padded = jnp.pad(field.astype(jnp.float32), 1)
        return upwind(padded, speed_x, speed_y).astype(jnp.bfloat16)
    propagated = lax.map(propagate_one, (spectrum, courant_x, courant_y))
    weights_all = jnp.concatenate([stress_weights, orbital_weights[None, :]], axis=0)

    def source_row(items):
        index, wind_row, wet_row = items
        row = lax.dynamic_index_in_dim(propagated, index, 1, keepdims=False)
        mixed = jnp.dot(transfer, row, preferred_element_type=jnp.float32)
        energy_row = row.astype(jnp.float32)
        total = jnp.dot(bin_width, energy_row, precision=lax.Precision.HIGHEST)
        ratio = total / (total + 1.0)
        part = energy_row + WAVE_STEP * (mixed - dissipation[:, None] * ratio[None, :] * energy_row)
        relaxed = part + WAVE_STEP * growth[:, None] * wind_row[None, :] * energy_row
        fresh = wet_row.astype(jnp.float32)[None, :] * jnp.maximum(relaxed, 0.0)
        forces = jnp.dot(weights_all, fresh, precision=lax.Precision.HIGHEST)
        return (fresh.astype(jnp.bfloat16), forces)
    rows_new, forces_rows = lax.map(source_row, (jnp.arange(GX, dtype=jnp.int32), wind, wave_wet))
    spectrum_new = jnp.transpose(rows_new, (1, 0, 2))
    forces = jnp.transpose(forces_rows, (1, 0, 2))
    forces = forces.reshape(3, N_TILE, ROWS_DEV, N_COMP, COLS_DEV).transpose(0, 1, 3, 2, 4)
    target = owner[..., 0]
    target_tile = target % N_TILE
    target_comp = target // N_TILE
    place = (target_tile * RR + cell_index // RC) * RY + target_comp * RC + cell_index % RC
    bottom = jnp.zeros((3, RX * RY), jnp.float32).at[:, place.reshape(-1).astype(jnp.int32)].add(forces.reshape(3, -1))
    bottom = bottom.reshape(3, RX, RY)
    shear_x = current_stress[0] + bottom[0]
    shear_y = current_stress[1] + bottom[1]
    shear = jnp.sqrt(shear_x * shear_x + shear_y * shear_y + bottom[2])
    low_share = 0.5 / NSED
    high_share = 1.0 - (NSED - 1) * low_share
    classes = jnp.arange(NSED, dtype=jnp.int32)[:, None, None]
    fraction = jnp.where(bed_class[None, :, :] == classes, high_share, low_share)
    erosion = class_props[0][:, None, None] * fraction * jnp.maximum(shear[None] / class_props[1][:, None, None] - 1.0, 0.0)
    wetness = roms_wet.astype(jnp.float32)
    settled = wetness * (sediment + SEDIMENT_STEP * (erosion - class_props[2][:, None, None] * sediment))
    carried = wetness * metals
    diffused = diffuse(jnp.concatenate([settled, carried], axis=0), wetness)
    sediment_new = diffused[:NSED]
    spread = diffused[NSED:]
    denominator = 1.0 + jnp.einsum('ms,sxy->mxy', partition, sediment_new, precision=lax.Precision.HIGHEST)
    dissolved = spread / denominator
    sorbed = spread - dissolved
    return (spectrum_new, sediment_new, dissolved, sorbed)
```

```python
import functools

import jax
import jax.numpy as jnp
from jax import lax
from jax.experimental import pallas as pl
from jax.experimental.pallas import tpu as pltpu
from jax.sharding import PartitionSpec as P

WAVE_STEP = 0.5
SEDIMENT_STEP = 1.0
DIFFUSION = 0.2
LANES = 128
PACK = 16
CHUNK = 4
PAIR = 2


def line(count, step):
    if step > 0:
        return [(i, i + 1) for i in range(count - 1)]
    return [(i + 1, i) for i in range(count - 1)]


def wave_kernel(
    n,
    n_tile,
    x_hbm,
    coef,
    transfer_hbm,
    bins,
    weights,
    damp,
    grow,
    wind,
    wet,
    out_hbm,
    forces,
    xs,
    send,
    recv,
    table,
    whole,
    acc,
    stage,
    in_sem,
    edge_send,
    edge_recv,
    table_sem,
    out_sem,
    send_sem,
    recv_sem,
):
    me = lax.axis_index("comp")
    tile = lax.axis_index("tile")
    rows, own, width = x_hbm.shape
    cols = width // n
    full = n * own
    chunks = rows // CHUNK
    pairs = rows // PAIR
    is_top, is_bottom = tile == 0, tile == n_tile - 1
    mesh_id = pl.DeviceIdType.MESH
    above = {"tile": lax.rem(tile + n_tile - 1, n_tile)}
    below = {"tile": lax.rem(tile + 1, n_tile)}

    def load(q):
        return pltpu.make_async_copy(
            x_hbm.at[pl.ds(q * CHUNK, CHUNK)],
            xs.at[pl.ds(1 + q * CHUNK, CHUNK)],
            in_sem.at[q],
        )

    for q in range(chunks):
        load(q).start()
    get_table = pltpu.make_async_copy(transfer_hbm, table.at[pl.ds(0, full)], table_sem.at[0])
    get_table.start()

    barrier = pltpu.get_barrier_semaphore()
    for o in range(1, n):
        pl.semaphore_signal(
            barrier, inc=1, device_id={"comp": lax.rem(me + o, n)}, device_id_type=mesh_id
        )

    @pl.when(jnp.logical_not(is_bottom))
    def _():
        pl.semaphore_signal(barrier, inc=1, device_id=below, device_id_type=mesh_id)

    @pl.when(jnp.logical_not(is_top))
    def _():
        pl.semaphore_signal(barrier, inc=1, device_id=above, device_id_type=mesh_id)

    ends = is_top.astype(jnp.int32) + is_bottom.astype(jnp.int32)
    pl.semaphore_wait(barrier, n + 1 - ends)

    to_below = pltpu.make_async_remote_copy(
        src_ref=x_hbm.at[pl.ds(rows - 1, 1)],
        dst_ref=xs.at[pl.ds(0, 1)],
        send_sem=edge_send.at[0],
        recv_sem=edge_recv.at[0],
        device_id=below,
        device_id_type=mesh_id,
    )
    to_above = pltpu.make_async_remote_copy(
        src_ref=x_hbm.at[pl.ds(0, 1)],
        dst_ref=xs.at[pl.ds(rows + 1, 1)],
        send_sem=edge_send.at[1],
        recv_sem=edge_recv.at[1],
        device_id=above,
        device_id_type=mesh_id,
    )

    @pl.when(jnp.logical_not(is_bottom))
    def _():
        to_below.start()

    @pl.when(jnp.logical_not(is_top))
    def _():
        to_above.start()

    @pl.when(is_top)
    def _():
        xs[0] = jnp.zeros((own, width), jnp.bfloat16)

    @pl.when(is_bottom)
    def _():
        xs[rows + 1] = jnp.zeros((own, width), jnp.bfloat16)

    def remote(q, o, source, target):
        return pltpu.make_async_remote_copy(
            src_ref=send.at[target, pl.ds(q * CHUNK, CHUNK)],
            dst_ref=recv.at[source, pl.ds(q * CHUNK, CHUNK)],
            send_sem=send_sem.at[o - 1, q],
            recv_sem=recv_sem.at[o - 1, q],
            device_id={"comp": target},
            device_id_type=mesh_id,
        )

    blocks, rest = own // PACK, own % PACK

    def upwind(row, part, size):
        lane = lax.broadcasted_iota(jnp.int32, (size, cols), 1)
        first_lane, last_lane = lane == 0, lane == cols - 1
        kept, from_north, from_south, from_west, from_east = [coef[i, part, :] for i in range(5)]

        def tile_of(at, d):
            return xs[at, part, d * cols : (d + 1) * cols].astype(jnp.float32)

        centre = [tile_of(row + 1, d) for d in range(n)]
        right = [pltpu.roll(c, 1, 1) for c in centre]
        left = [pltpu.roll(c, cols - 1, 1) for c in centre]
        nothing = jnp.zeros((size, cols), jnp.float32)
        for d in range(n):
            west = jnp.where(first_lane, right[d - 1] if d else nothing, right[d])
            east = jnp.where(last_lane, left[d + 1] if d < n - 1 else nothing, left[d])
            moved = (
                kept * centre[d]
                + from_north * tile_of(row, d)
                + from_south * tile_of(row + 2, d)
                + from_west * west
                + from_east * east
            )
            send[d, row, part, :] = moved.astype(jnp.bfloat16)

    load(0).wait()
    load(1).wait()

    @pl.loop(0, chunks)
    def _(step):
        q = lax.rem(step + 1, chunks)

        @pl.when(step < chunks - 2)
        def _():
            load(q + 1).wait()

        @pl.when(jnp.logical_and(step == chunks - 2, jnp.logical_not(is_bottom)))
        def _():
            to_above.wait_recv()

        @pl.when(jnp.logical_and(step == chunks - 1, jnp.logical_not(is_top)))
        def _():
            to_below.wait_recv()

        @pl.loop(0, CHUNK * blocks)
        def _(i):
            start = pl.multiple_of(lax.rem(i, blocks) * PACK, PACK)
            upwind(q * CHUNK + i // blocks, pl.ds(start, PACK), PACK)

        if rest:

            @pl.loop(0, CHUNK)
            def _(i):
                upwind(q * CHUNK + i, pl.ds(blocks * PACK, rest), rest)

        for o in range(1, n):
            remote(q, o, me, lax.rem(me + o, n)).start()
        here = pl.ds(q * CHUNK, CHUNK)
        recv[me, here] = send[me, here]

    get_table.wait()
    table[full : full + PACK, :] = bins[...]

    def put(i, slot):
        return pltpu.make_async_copy(
            stage.at[slot], out_hbm.at[pl.ds(i * PAIR, PAIR)], out_sem.at[slot]
        )

    band = 3 * PACK if full % (3 * PACK) == 0 else PACK

    def mix(i, slot, is_first):
        row = i * PAIR
        for s in range(n):
            for a in range(PAIR):
                whole[s * own : (s + 1) * own, a * cols : (a + 1) * cols] = recv[
                    s, row + a
                ].astype(jnp.float32)
        acc[...] = jnp.dot(
            table[...], whole[...].astype(jnp.bfloat16), preferred_element_type=jnp.float32
        )
        total = acc[full : full + 1, :] + acc[full + 1 : full + 2, :]
        ratio = total / (total + 1.0)
        gust = jnp.concatenate([wind[pl.ds(row + a, 1), :] for a in range(PAIR)], axis=1)
        open_water = jnp.concatenate([wet[pl.ds(row + a, 1), :] for a in range(PAIR)], axis=1)

        @pl.when(jnp.logical_not(is_first))
        def _():
            put(i, slot).wait()

        @pl.loop(0, full // band)
        def _(b):
            part = pl.ds(pl.multiple_of(b * band, band), band)
            damping, growing = damp[part, :], grow[part, :]
            for a in range(PAIR):
                span = slice(a * cols, (a + 1) * cols)
                gain = 1.0 - damping * ratio[:, span] + growing * gust[:, span]
                relaxed = WAVE_STEP * acc[part, span] + whole[part, span] * gain
                fresh = open_water[:, span] * jnp.maximum(relaxed, 0.0)
                stage[slot, a, part, :] = fresh.astype(jnp.bfloat16)

        fresh_all = jnp.concatenate([stage[slot, a] for a in range(PAIR)], axis=1)
        pulled = jnp.dot(weights[...], fresh_all, preferred_element_type=jnp.float32)
        for a in range(PAIR):
            forces[row + a] = pulled[:, a * cols : (a + 1) * cols]
        put(i, slot).start()

    per_chunk = CHUNK // PAIR

    @pl.loop(0, chunks)
    def _(step):
        q = lax.rem(step + 1, chunks)
        for o in range(1, n):
            remote(q, o, lax.rem(me + n - o, n), me).wait_recv()
        for a in range(per_chunk):
            mix(q * per_chunk + a, a % 2, step == 0)

    for a in range(2):
        put(a, a).wait()

    @pl.when(jnp.logical_not(is_bottom))
    def _():
        to_below.wait_send()

    @pl.when(jnp.logical_not(is_top))
    def _():
        to_above.wait_send()

    @pl.loop(0, chunks)
    def _(q):
        for o in range(1, n):
            remote(q, o, me, lax.rem(me + o, n)).wait_send()


def split_two(values):
    high = values.astype(jnp.bfloat16)
    low = (values - high.astype(jnp.float32)).astype(jnp.bfloat16)
    return high, low


def on_device(
    spectrum,
    courant_x,
    courant_y,
    growth,
    dissipation,
    bin_width,
    transfer,
    stress_weights,
    orbital_weights,
    wind,
    wave_wet,
    owner,
    cell_index,
    current_stress,
    sediment,
    metals,
    bed_class,
    roms_wet,
    class_props,
    partition,
):
    n_comp = lax.axis_size("comp")
    n_tile = lax.axis_size("tile")
    devices = n_comp * n_tile
    own_count, rows, width = spectrum.shape
    cols = width // n_comp
    count = n_comp * own_count
    bf16, f32 = jnp.bfloat16, jnp.float32

    by_row = jnp.transpose(spectrum, (1, 0, 2))
    first = lax.axis_index("comp") * own_count
    speed_x = lax.dynamic_slice_in_dim(courant_x, first, own_count)
    speed_y = lax.dynamic_slice_in_dim(courant_y, first, own_count)
    coef = jnp.stack(
        [
            1.0 - jnp.abs(speed_x) - jnp.abs(speed_y),
            jnp.maximum(speed_x, 0.0),
            -jnp.minimum(speed_x, 0.0),
            jnp.maximum(speed_y, 0.0),
            -jnp.minimum(speed_y, 0.0),
        ]
    )
    coef = jnp.broadcast_to(coef[:, :, None], (5, own_count, cols))
    bins = jnp.pad(jnp.stack(split_two(bin_width)), ((0, PACK - 2), (0, 0)))
    weights_all = jnp.concatenate([stress_weights, orbital_weights[None, :]], axis=0)
    weights = jnp.pad(jnp.concatenate(split_two(weights_all), axis=0), ((0, PACK - 6), (0, 0)))
    damp = jnp.broadcast_to((WAVE_STEP * dissipation)[:, None], (count, cols))
    grow = jnp.broadcast_to((WAVE_STEP * growth)[:, None], (count, cols))

    vmem = pl.BlockSpec(memory_space=pltpu.VMEM)
    hbm = pl.BlockSpec(memory_space=pl.ANY)
    chunks = rows // CHUNK
    fresh, pulled = pl.pallas_call(
        functools.partial(wave_kernel, n_comp, n_tile),
        out_shape=(
            jax.ShapeDtypeStruct((rows, count, cols), bf16),
            jax.ShapeDtypeStruct((rows, PACK, cols), f32),
        ),
        in_specs=[hbm, vmem, hbm] + [vmem] * 6,
        out_specs=(hbm, vmem),
        scratch_shapes=[
            pltpu.VMEM((rows + 2, own_count, width), bf16),
            pltpu.VMEM((n_comp, rows, own_count, cols), bf16),
            pltpu.VMEM((n_comp, rows, own_count, cols), bf16),
            pltpu.VMEM((count + PACK, count), bf16),
            pltpu.VMEM((count, PAIR * cols), f32),
            pltpu.VMEM((count + PACK, PAIR * cols), f32),
            pltpu.VMEM((2, PAIR, count, cols), bf16),
            pltpu.SemaphoreType.DMA((chunks,)),
            pltpu.SemaphoreType.DMA((2,)),
            pltpu.SemaphoreType.DMA((2,)),
            pltpu.SemaphoreType.DMA((1,)),
            pltpu.SemaphoreType.DMA((2,)),
            pltpu.SemaphoreType.DMA((n_comp - 1, chunks)),
            pltpu.SemaphoreType.DMA((n_comp - 1, chunks)),
        ],
        compiler_params=pltpu.CompilerParams(
            collective_id=0, has_side_effects=True, vmem_limit_bytes=63000 * 1024
        ),
    )(by_row, coef, transfer, bins, weights, damp, grow, wind, wave_wet.astype(f32))
    spectrum_new = jnp.transpose(fresh, (1, 0, 2))
    forces = pulled[:, :3] + pulled[:, 3:6]

    points = rows * cols
    slots = max(2, 3 * points // devices)
    cells_r, cells_c = sediment.shape[1], sediment.shape[2]
    owner_rc = owner.reshape(rows, cols)
    cell_rc = cell_index.reshape(rows, cols)
    hit = owner_rc[None] == jnp.arange(devices, dtype=jnp.int32)[:, None, None]
    hits = hit.astype(bf16)
    before_col = (jnp.arange(cols)[:, None] < jnp.arange(cols)[None, :]).astype(bf16)
    before_row = (jnp.arange(rows)[:, None] < jnp.arange(rows)[None, :]).astype(bf16)
    in_row = jnp.einsum("orc,cd->ord", hits, before_col, preferred_element_type=f32)
    row_sum = jnp.sum(hits.astype(f32), axis=2).astype(bf16)
    above = jnp.einsum("or,rs->os", row_sum, before_row, preferred_element_type=f32)
    rank = jnp.sum(jnp.where(hit, in_row + above[:, :, None], 0.0), axis=0).reshape(points)
    placed = (
        rank.astype(jnp.int32)[None, :] == jnp.arange(slots, dtype=jnp.int32)[:, None]
    ).astype(bf16)
    items = jnp.concatenate(
        [
            jnp.transpose(forces, (1, 0, 2)).astype(bf16),
            (cell_rc // cells_c).astype(bf16)[None],
            (cell_rc % cells_c).astype(bf16)[None],
        ],
        axis=0,
    ).reshape(5, 1, points)
    spreaded = (items * hits.reshape(1, devices, points)).reshape(5 * devices, points)
    packed = lax.dot_general(
        spreaded, placed, (((1,), (1,)), ((), ())), preferred_element_type=f32
    ).astype(bf16)
    got = lax.all_to_all(
        packed.reshape(5, devices, slots), ("comp", "tile"), split_axis=1, concat_axis=1, tiled=True
    ).reshape(5, devices * slots)
    at_row = got[3][None, :] == jnp.arange(cells_r, dtype=jnp.int32).astype(bf16)[:, None]
    at_col = got[4][None, :] == jnp.arange(cells_c, dtype=jnp.int32).astype(bf16)[:, None]
    lifted = jnp.where(at_row[None], got[:3, None, :], jnp.zeros((), bf16))
    bottom = lax.dot_general(
        lifted.reshape(3 * cells_r, devices * slots),
        at_col.astype(bf16),
        (((1,), (1,)), ((), ())),
        preferred_element_type=f32,
    ).reshape(3, cells_r, cells_c)

    shear_x = current_stress[0] + bottom[0]
    shear_y = current_stress[1] + bottom[1]
    shear = jnp.sqrt(shear_x * shear_x + shear_y * shear_y + bottom[2])
    classes_count = sediment.shape[0]
    low_share = 0.5 / classes_count
    high_share = 1.0 - (classes_count - 1) * low_share
    classes = jnp.arange(classes_count, dtype=jnp.int32)[:, None, None]
    fraction = jnp.where(bed_class[None] == classes, high_share, low_share)
    erosion = (
        class_props[0][:, None, None]
        * fraction
        * jnp.maximum(shear[None] / class_props[1][:, None, None] - 1.0, 0.0)
    )
    wetness = roms_wet.astype(f32)
    settled = wetness * (
        sediment + SEDIMENT_STEP * (erosion - class_props[2][:, None, None] * sediment)
    )
    carried = wetness * metals
    fields = jnp.concatenate([settled, carried], axis=0)
    from_north = lax.ppermute(fields[:, -1:, :], "tile", line(n_tile, 1))
    from_south = lax.ppermute(fields[:, :1, :], "tile", line(n_tile, -1))
    from_west = lax.ppermute(fields[:, :, -1:], "comp", line(n_comp, 1))
    from_east = lax.ppermute(fields[:, :, :1], "comp", line(n_comp, -1))
    tall = jnp.concatenate([from_north, fields, from_south], axis=1)
    wide = jnp.concatenate([from_west, fields, from_east], axis=2)
    beside_all = tall[:, :-2] + tall[:, 2:] + wide[:, :, :-2] + wide[:, :, 2:]
    diffused = wetness * (fields + DIFFUSION * (beside_all - 4.0 * fields))
    sediment_new = diffused[:classes_count]
    spread_new = diffused[classes_count:]
    denominator = 1.0 + jnp.sum(partition[:, :, None, None] * sediment_new[None], axis=1)
    dissolved = spread_new / denominator
    sorbed = spread_new - dissolved
    return (spectrum_new, sediment_new, dissolved, sorbed)


def solution(mesh):
    in_specs = (
        P("comp", "tile", None),
        P(),
        P(),
        P(),
        P(),
        P(),
        P(),
        P(),
        P(),
        P("tile", "comp"),
        P("tile", "comp"),
        P("tile", "comp", None, None, None),
        P("tile", "comp", None, None),
        P(None, "tile", "comp"),
        P(None, "tile", "comp"),
        P(None, "tile", "comp"),
        P("tile", "comp"),
        P("tile", "comp"),
        P(),
        P(),
    )
    out_specs = (
        P(None, "tile", "comp"),
        P(None, "tile", "comp"),
        P(None, "tile", "comp"),
        P(None, "tile", "comp"),
    )
    return jax.shard_map(
        on_device, mesh=mesh, in_specs=in_specs, out_specs=out_specs, check_vma=False
    )
```

```python
import functools

import jax
import jax.numpy as jnp
from jax import lax
from jax.experimental import pallas as pl
from jax.experimental.pallas import tpu as pltpu
from jax.sharding import PartitionSpec as P

WAVE_STEP = 0.5
SEDIMENT_STEP = 1.0
DIFFUSION = 0.2
LANES = 128
PACK = 16
CHUNK = 4
PAIR = 2


def line(count, step):
    if step > 0:
        return [(i, i + 1) for i in range(count - 1)]
    return [(i + 1, i) for i in range(count - 1)]


def wave_kernel(
    n,
    n_tile,
    x_hbm,
    coef,
    transfer_hbm,
    bins,
    weights,
    damp,
    grow,
    wind,
    wet,
    out_hbm,
    forces,
    xs,
    send,
    recv,
    table,
    whole,
    acc,
    stage,
    in_sem,
    edge_send,
    edge_recv,
    table_sem,
    out_sem,
    send_sem,
    recv_sem,
):
    me = lax.axis_index("comp")
    tile = lax.axis_index("tile")
    rows, own, width = x_hbm.shape
    cols = width // n
    full = n * own
    chunks = rows // CHUNK
    pairs = rows // PAIR
    is_top, is_bottom = tile == 0, tile == n_tile - 1
    mesh_id = pl.DeviceIdType.MESH
    above = {"tile": lax.rem(tile + n_tile - 1, n_tile)}
    below = {"tile": lax.rem(tile + 1, n_tile)}

    def load(q):
        return pltpu.make_async_copy(
            x_hbm.at[pl.ds(q * CHUNK, CHUNK)],
            xs.at[pl.ds(1 + q * CHUNK, CHUNK)],
            in_sem.at[q],
        )

    for q in range(chunks):
        load(q).start()
    get_table = pltpu.make_async_copy(transfer_hbm, table.at[pl.ds(0, full)], table_sem.at[0])
    get_table.start()

    barrier = pltpu.get_barrier_semaphore()
    for o in range(1, n):
        pl.semaphore_signal(
            barrier, inc=1, device_id={"comp": lax.rem(me + o, n)}, device_id_type=mesh_id
        )

    @pl.when(jnp.logical_not(is_bottom))
    def _():
        pl.semaphore_signal(barrier, inc=1, device_id=below, device_id_type=mesh_id)

    @pl.when(jnp.logical_not(is_top))
    def _():
        pl.semaphore_signal(barrier, inc=1, device_id=above, device_id_type=mesh_id)

    ends = is_top.astype(jnp.int32) + is_bottom.astype(jnp.int32)
    pl.semaphore_wait(barrier, n + 1 - ends)

    to_below = pltpu.make_async_remote_copy(
        src_ref=x_hbm.at[pl.ds(rows - 1, 1)],
        dst_ref=xs.at[pl.ds(0, 1)],
        send_sem=edge_send.at[0],
        recv_sem=edge_recv.at[0],
        device_id=below,
        device_id_type=mesh_id,
    )
    to_above = pltpu.make_async_remote_copy(
        src_ref=x_hbm.at[pl.ds(0, 1)],
        dst_ref=xs.at[pl.ds(rows + 1, 1)],
        send_sem=edge_send.at[1],
        recv_sem=edge_recv.at[1],
        device_id=above,
        device_id_type=mesh_id,
    )

    @pl.when(jnp.logical_not(is_bottom))
    def _():
        to_below.start()

    @pl.when(jnp.logical_not(is_top))
    def _():
        to_above.start()

    @pl.when(is_top)
    def _():
        xs[0] = jnp.zeros((own, width), jnp.bfloat16)

    @pl.when(is_bottom)
    def _():
        xs[rows + 1] = jnp.zeros((own, width), jnp.bfloat16)

    def remote(q, o, source, target):
        return pltpu.make_async_remote_copy(
            src_ref=send.at[target, pl.ds(q * CHUNK, CHUNK)],
            dst_ref=recv.at[source, pl.ds(q * CHUNK, CHUNK)],
            send_sem=send_sem.at[o - 1, q],
            recv_sem=recv_sem.at[o - 1, q],
            device_id={"comp": target},
            device_id_type=mesh_id,
        )

    blocks, rest = own // PACK, own % PACK

    def upwind(row, part, size):
        lane = lax.broadcasted_iota(jnp.int32, (size, cols), 1)
        first_lane, last_lane = lane == 0, lane == cols - 1
        kept, from_north, from_south, from_west, from_east = [coef[i, part, :] for i in range(5)]

        def tile_of(at, d):
            return xs[at, part, d * cols : (d + 1) * cols].astype(jnp.float32)

        centre = [tile_of(row + 1, d) for d in range(n)]
        right = [pltpu.roll(c, 1, 1) for c in centre]
        left = [pltpu.roll(c, cols - 1, 1) for c in centre]
        nothing = jnp.zeros((size, cols), jnp.float32)
        for d in range(n):
            west = jnp.where(first_lane, right[d - 1] if d else nothing, right[d])
            east = jnp.where(last_lane, left[d + 1] if d < n - 1 else nothing, left[d])
            moved = (
                kept * centre[d]
                + from_north * tile_of(row, d)
                + from_south * tile_of(row + 2, d)
                + from_west * west
                + from_east * east
            )
            send[d, row, part, :] = moved.astype(jnp.bfloat16)

    load(0).wait()
    load(1).wait()

    @pl.loop(0, chunks)
    def _(step):
        q = lax.rem(step + 1, chunks)

        @pl.when(step < chunks - 2)
        def _():
            load(q + 1).wait()

        @pl.when(jnp.logical_and(step == chunks - 2, jnp.logical_not(is_bottom)))
        def _():
            to_above.wait_recv()

        @pl.when(jnp.logical_and(step == chunks - 1, jnp.logical_not(is_top)))
        def _():
            to_below.wait_recv()

        @pl.loop(0, CHUNK * blocks)
        def _(i):
            start = pl.multiple_of(lax.rem(i, blocks) * PACK, PACK)
            upwind(q * CHUNK + i // blocks, pl.ds(start, PACK), PACK)

        if rest:

            @pl.loop(0, CHUNK)
            def _(i):
                upwind(q * CHUNK + i, pl.ds(blocks * PACK, rest), rest)

        for o in range(1, n):
            remote(q, o, me, lax.rem(me + o, n)).start()
        here = pl.ds(q * CHUNK, CHUNK)
        recv[me, here] = send[me, here]

    get_table.wait()
    table[full : full + PACK, :] = bins[...]

    def put(i, slot):
        return pltpu.make_async_copy(
            stage.at[slot], out_hbm.at[pl.ds(i * PAIR, PAIR)], out_sem.at[slot]
        )

    band = 3 * PACK if full % (3 * PACK) == 0 else PACK

    def mix(i, slot, is_first):
        row = i * PAIR
        for s in range(n):
            for a in range(PAIR):
                whole[s * own : (s + 1) * own, a * cols : (a + 1) * cols] = recv[
                    s, row + a
                ].astype(jnp.float32)
        acc[...] = jnp.dot(
            table[...], whole[...].astype(jnp.bfloat16), preferred_element_type=jnp.float32
        )
        total = acc[full : full + 1, :] + acc[full + 1 : full + 2, :]
        ratio = total / (total + 1.0)
        gust = jnp.concatenate([wind[pl.ds(row + a, 1), :] for a in range(PAIR)], axis=1)
        open_water = jnp.concatenate([wet[pl.ds(row + a, 1), :] for a in range(PAIR)], axis=1)

        @pl.when(jnp.logical_not(is_first))
        def _():
            put(i, slot).wait()

        @pl.loop(0, full // band)
        def _(b):
            part = pl.ds(pl.multiple_of(b * band, band), band)
            damping, growing = damp[part, :], grow[part, :]
            for a in range(PAIR):
                span = slice(a * cols, (a + 1) * cols)
                gain = 1.0 - damping * ratio[:, span] + growing * gust[:, span]
                relaxed = WAVE_STEP * acc[part, span] + whole[part, span] * gain
                fresh = open_water[:, span] * jnp.maximum(relaxed, 0.0)
                stage[slot, a, part, :] = fresh.astype(jnp.bfloat16)

        fresh_all = jnp.concatenate([stage[slot, a] for a in range(PAIR)], axis=1)
        pulled = jnp.dot(weights[...], fresh_all, preferred_element_type=jnp.float32)
        for a in range(PAIR):
            forces[row + a] = pulled[:, a * cols : (a + 1) * cols]
        put(i, slot).start()

    per_chunk = CHUNK // PAIR

    @pl.loop(0, chunks)
    def _(step):
        q = lax.rem(step + 1, chunks)
        for o in range(1, n):
            remote(q, o, lax.rem(me + n - o, n), me).wait_recv()
        for a in range(per_chunk):
            mix(q * per_chunk + a, a % 2, step == 0)

    for a in range(2):
        put(a, a).wait()

    @pl.when(jnp.logical_not(is_bottom))
    def _():
        to_below.wait_send()

    @pl.when(jnp.logical_not(is_top))
    def _():
        to_above.wait_send()

    @pl.loop(0, chunks)
    def _(q):
        for o in range(1, n):
            remote(q, o, me, lax.rem(me + o, n)).wait_send()


def reorder_kernel(x, out, held):
    rows, band, cols = x.shape
    for i in range(rows):
        held[pl.ds(i, band, stride=rows), :] = x[i].astype(jnp.float32)
    out[...] = held[...].reshape(band, rows, cols).astype(jnp.bfloat16)


def reorder(fresh):
    rows, count, cols = fresh.shape
    band = 3 * PACK if count % (3 * PACK) == 0 else PACK
    return pl.pallas_call(
        reorder_kernel,
        out_shape=jax.ShapeDtypeStruct((count, rows, cols), jnp.bfloat16),
        grid=(count // band,),
        in_specs=[pl.BlockSpec((rows, band, cols), lambda i: (0, i, 0))],
        out_specs=pl.BlockSpec((band, rows, cols), lambda i: (i, 0, 0)),
        scratch_shapes=[pltpu.VMEM((band * rows, cols), jnp.float32)],
        cost_estimate=pl.CostEstimate(
            flops=fresh.size, bytes_accessed=4 * fresh.size, transcendentals=0
        ),
    )(fresh)


def split_two(values):
    high = values.astype(jnp.bfloat16)
    low = (values - high.astype(jnp.float32)).astype(jnp.bfloat16)
    return high, low


def on_device(
    spectrum,
    courant_x,
    courant_y,
    growth,
    dissipation,
    bin_width,
    transfer,
    stress_weights,
    orbital_weights,
    wind,
    wave_wet,
    owner,
    cell_index,
    current_stress,
    sediment,
    metals,
    bed_class,
    roms_wet,
    class_props,
    partition,
):
    n_comp = lax.axis_size("comp")
    n_tile = lax.axis_size("tile")
    devices = n_comp * n_tile
    own_count, rows, width = spectrum.shape
    cols = width // n_comp
    count = n_comp * own_count
    bf16, f32 = jnp.bfloat16, jnp.float32

    by_row = jnp.transpose(spectrum, (1, 0, 2))
    first = lax.axis_index("comp") * own_count
    speed_x = lax.dynamic_slice_in_dim(courant_x, first, own_count)
    speed_y = lax.dynamic_slice_in_dim(courant_y, first, own_count)
    coef = jnp.stack(
        [
            1.0 - jnp.abs(speed_x) - jnp.abs(speed_y),
            jnp.maximum(speed_x, 0.0),
            -jnp.minimum(speed_x, 0.0),
            jnp.maximum(speed_y, 0.0),
            -jnp.minimum(speed_y, 0.0),
        ]
    )
    coef = jnp.broadcast_to(coef[:, :, None], (5, own_count, cols))
    bins = jnp.pad(jnp.stack(split_two(bin_width)), ((0, PACK - 2), (0, 0)))
    weights_all = jnp.concatenate([stress_weights, orbital_weights[None, :]], axis=0)
    weights = jnp.pad(jnp.concatenate(split_two(weights_all), axis=0), ((0, PACK - 6), (0, 0)))
    damp = jnp.broadcast_to((WAVE_STEP * dissipation)[:, None], (count, cols))
    grow = jnp.broadcast_to((WAVE_STEP * growth)[:, None], (count, cols))

    vmem = pl.BlockSpec(memory_space=pltpu.VMEM)
    hbm = pl.BlockSpec(memory_space=pl.ANY)
    chunks = rows // CHUNK
    fresh, pulled = pl.pallas_call(
        functools.partial(wave_kernel, n_comp, n_tile),
        out_shape=(
            jax.ShapeDtypeStruct((rows, count, cols), bf16),
            jax.ShapeDtypeStruct((rows, PACK, cols), f32),
        ),
        in_specs=[hbm, vmem, hbm] + [vmem] * 6,
        out_specs=(hbm, vmem),
        scratch_shapes=[
            pltpu.VMEM((rows + 2, own_count, width), bf16),
            pltpu.VMEM((n_comp, rows, own_count, cols), bf16),
            pltpu.VMEM((n_comp, rows, own_count, cols), bf16),
            pltpu.VMEM((count + PACK, count), bf16),
            pltpu.VMEM((count, PAIR * cols), f32),
            pltpu.VMEM((count + PACK, PAIR * cols), f32),
            pltpu.VMEM((2, PAIR, count, cols), bf16),
            pltpu.SemaphoreType.DMA((chunks,)),
            pltpu.SemaphoreType.DMA((2,)),
            pltpu.SemaphoreType.DMA((2,)),
            pltpu.SemaphoreType.DMA((1,)),
            pltpu.SemaphoreType.DMA((2,)),
            pltpu.SemaphoreType.DMA((n_comp - 1, chunks)),
            pltpu.SemaphoreType.DMA((n_comp - 1, chunks)),
        ],
        compiler_params=pltpu.CompilerParams(
            collective_id=0, has_side_effects=True, vmem_limit_bytes=63000 * 1024
        ),
    )(by_row, coef, transfer, bins, weights, damp, grow, wind, wave_wet.astype(f32))
    spectrum_new = reorder(fresh)
    forces = pulled[:, :3] + pulled[:, 3:6]

    points = rows * cols
    slots = max(2, 3 * points // devices)
    cells_r, cells_c = sediment.shape[1], sediment.shape[2]
    owner_rc = owner.reshape(rows, cols)
    cell_rc = cell_index.reshape(rows, cols)
    hit = owner_rc[None] == jnp.arange(devices, dtype=jnp.int32)[:, None, None]
    hits = hit.astype(bf16)
    before_col = (jnp.arange(cols)[:, None] < jnp.arange(cols)[None, :]).astype(bf16)
    before_row = (jnp.arange(rows)[:, None] < jnp.arange(rows)[None, :]).astype(bf16)
    in_row = jnp.einsum("orc,cd->ord", hits, before_col, preferred_element_type=f32)
    row_sum = jnp.sum(hits.astype(f32), axis=2).astype(bf16)
    above = jnp.einsum("or,rs->os", row_sum, before_row, preferred_element_type=f32)
    rank = jnp.sum(jnp.where(hit, in_row + above[:, :, None], 0.0), axis=0).reshape(points)
    placed = (
        rank.astype(jnp.int32)[None, :] == jnp.arange(slots, dtype=jnp.int32)[:, None]
    ).astype(bf16)
    items = jnp.concatenate(
        [
            jnp.transpose(forces, (1, 0, 2)).astype(bf16),
            (cell_rc // cells_c).astype(bf16)[None],
            (cell_rc % cells_c).astype(bf16)[None],
        ],
        axis=0,
    ).reshape(5, 1, points)
    spreaded = (items * hits.reshape(1, devices, points)).reshape(5 * devices, points)
    packed = lax.dot_general(
        spreaded, placed, (((1,), (1,)), ((), ())), preferred_element_type=f32
    ).astype(bf16)
    got = lax.all_to_all(
        packed.reshape(5, devices, slots), ("comp", "tile"), split_axis=1, concat_axis=1, tiled=True
    )
    got, spectrum_new = lax.optimization_barrier((got, spectrum_new))
    got = got.reshape(5, devices * slots)
    at_row = got[3][None, :] == jnp.arange(cells_r, dtype=jnp.int32).astype(bf16)[:, None]
    at_col = got[4][None, :] == jnp.arange(cells_c, dtype=jnp.int32).astype(bf16)[:, None]
    lifted = jnp.where(at_row[None], got[:3, None, :], jnp.zeros((), bf16))
    bottom = lax.dot_general(
        lifted.reshape(3 * cells_r, devices * slots),
        at_col.astype(bf16),
        (((1,), (1,)), ((), ())),
        preferred_element_type=f32,
    ).reshape(3, cells_r, cells_c)

    shear_x = current_stress[0] + bottom[0]
    shear_y = current_stress[1] + bottom[1]
    shear = jnp.sqrt(shear_x * shear_x + shear_y * shear_y + bottom[2])
    classes_count = sediment.shape[0]
    low_share = 0.5 / classes_count
    high_share = 1.0 - (classes_count - 1) * low_share
    classes = jnp.arange(classes_count, dtype=jnp.int32)[:, None, None]
    fraction = jnp.where(bed_class[None] == classes, high_share, low_share)
    erosion = (
        class_props[0][:, None, None]
        * fraction
        * jnp.maximum(shear[None] / class_props[1][:, None, None] - 1.0, 0.0)
    )
    wetness = roms_wet.astype(f32)
    settled = wetness * (
        sediment + SEDIMENT_STEP * (erosion - class_props[2][:, None, None] * sediment)
    )
    carried = wetness * metals
    fields = jnp.concatenate([settled, carried], axis=0)
    from_north = lax.ppermute(fields[:, -1:, :], "tile", line(n_tile, 1))
    from_south = lax.ppermute(fields[:, :1, :], "tile", line(n_tile, -1))
    from_west = lax.ppermute(fields[:, :, -1:], "comp", line(n_comp, 1))
    from_east = lax.ppermute(fields[:, :, :1], "comp", line(n_comp, -1))
    tall = jnp.concatenate([from_north, fields, from_south], axis=1)
    wide = jnp.concatenate([from_west, fields, from_east], axis=2)
    beside_all = tall[:, :-2] + tall[:, 2:] + wide[:, :, :-2] + wide[:, :, 2:]
    diffused = wetness * (fields + DIFFUSION * (beside_all - 4.0 * fields))
    sediment_new = diffused[:classes_count]
    spread_new = diffused[classes_count:]
    denominator = 1.0 + jnp.sum(partition[:, :, None, None] * sediment_new[None], axis=1)
    dissolved = spread_new / denominator
    sorbed = spread_new - dissolved
    return (spectrum_new, sediment_new, dissolved, sorbed)


def solution(mesh):
    in_specs = (
        P("comp", "tile", None),
        P(),
        P(),
        P(),
        P(),
        P(),
        P(),
        P(),
        P(),
        P("tile", "comp"),
        P("tile", "comp"),
        P("tile", "comp", None, None, None),
        P("tile", "comp", None, None),
        P(None, "tile", "comp"),
        P(None, "tile", "comp"),
        P(None, "tile", "comp"),
        P("tile", "comp"),
        P("tile", "comp"),
        P(),
        P(),
    )
    out_specs = (
        P(None, "tile", "comp"),
        P(None, "tile", "comp"),
        P(None, "tile", "comp"),
        P(None, "tile", "comp"),
    )
    return jax.shard_map(
        on_device, mesh=mesh, in_specs=in_specs, out_specs=out_specs, check_vma=False
    )
```
